32 devices in a mesh: groups: 2 (over y), tm: 4 (over z), space: 2 (over x), chan: 2 (over core).
Axes of the slice: x: 2, y: 2, z: 4, core: 2. Of those that a mesh axis runs over, the one named last changes fastest.
Arguments:
- activations: bfloat16 [256, 8, 16, 256], P(('groups', 'chan'), 'tm', 'space'), parts along dimension 0
- frame_clip: int32 [16], P(('groups', 'tm')), parts along dimension 0, may hold values from 0 to 3, as said below
- conv_weight: bfloat16 [3, 3, 3, 128, 128], replicated, may hold values from -0.109375 to 0.109375
- norm_gain: float32 [128], replicated, may hold values from 0.25 to 1.75
- norm_bias: float32 [128], replicated, may hold values from -3 to 3
- out_weight: bfloat16 [2, 2, 128, 32], replicated, may hold values from -0.25 to 0.25
- owner: int32 [4, 32, 1], P(('groups', 'space'), 'tm'), parts along dimension 0, may hold values from 0 to 3; in each aligned block of 8 rows (0 to 7, 8 to 15, ..., all dimensions but the last counted through in order) at most 4 rows name the same one
Outputs:
- owned: bfloat16 [4, 64, 32, 128], P(('groups', 'space'), 'tm', 'chan'), parts along dimension 0
The draws below stay inside these ranges and needn't reach their ends.
There are 2 independent parts, one for each index of `groups`. The reference program is written for one: setup_inputs(seed, part) draws one part's arguments, and reference() takes and returns one part's arrays. A program takes and returns all parts, laid end to end along the dimension named above; an argument that names none is the same for every part. Nothing has to cross between parts.
Inputs may be any that keep to these rules, and one draw needn't show every extreme that they name: `frame_clip`: clip numbers never fall along the frames; each clip has 1 to 4 frames and one has exactly 4. Among the 8 rows of one tm index (aligned blocks), no owner is named more than 4 times; some owner is named exactly 4 times in some block.
All inputs are finite; a program needn't handle non-finite values.
Results may differ from the reference program's by a relative error of at most 0.012.
Values may be sent and summed in bfloat16 or wider, within the bound.
A program may use at most 64 MiB of HBM per device.

```python
import math
import jax
import jax.numpy as jnp
import numpy as np
from jax import lax

CHANNELS = 128
GROUPS = 32
COLUMNS = 256
CLIPS = 4
MOMENTS = 32
HALF_ROWS = 4
HALF_COLS = 128
SEND_ROWS = 8
FRAMES = 8
HEIGHT = 16
LONGEST = 4
CAPACITY = 4
N_TM = 4
N_SPACE = 2


def draw_activations(key, part):
    key_base, key_rows, key_chan = jax.random.split(key, 3)
    frame_pos = jnp.arange(FRAMES, dtype=jnp.float32) / max(FRAMES - 1, 1)
    frame_scale = jnp.exp(jnp.log(3.0) * frame_pos)
    shape = (CHANNELS, FRAMES, HEIGHT, COLUMNS)
    base = jnp.clip(jax.random.normal(key_base, shape, jnp.float32), -6.0, 6.0)
    row_scale = jnp.exp(jax.random.uniform(key_rows, (1, FRAMES, HEIGHT, 1), jnp.float32, jnp.log(0.5), jnp.log(5.0)))
    chan_scale = jnp.exp(jax.random.uniform(key_chan, (CHANNELS, 1, 1, 1), jnp.float32, jnp.log(0.5), jnp.log(2.0)))
    return (base * row_scale * chan_scale * frame_scale[None, :, None, None]).astype(jnp.bfloat16)


def draw_frame_clip(key, part):
    key_cuts, key_place = jax.random.split(jax.random.fold_in(key, 7), 2)
    remain = FRAMES - LONGEST
    picked = jax.random.permutation(key_cuts, remain - 1)[:CLIPS - 2] + 1
    cuts = jnp.sort(picked).astype(jnp.int32)
    bounds = jnp.concatenate([jnp.zeros((1,), jnp.int32), cuts, jnp.full((1,), remain, jnp.int32)])
    others = bounds[1:] - bounds[:-1]
    place = jax.random.randint(key_place, (), 0, CLIPS, dtype=jnp.int32)
    index = jnp.arange(CLIPS, dtype=jnp.int32)
    other_index = jnp.clip(index - (index > place).astype(jnp.int32), 0, CLIPS - 2)
    lengths = jnp.where(index == place, LONGEST, others[other_index]).astype(jnp.int32)
    ends = jnp.cumsum(lengths).astype(jnp.int32)
    frames = jnp.arange(FRAMES, dtype=jnp.int32)
    return jnp.sum((frames[:, None] >= ends[None, :CLIPS - 1]).astype(jnp.int32), axis=1).astype(jnp.int32)


def shared_out(rng, own, number, rows, count, top, bound, slope):
    ranking = jax.random.permutation(rng, count)
    heavy_load, usual = load_shares(count, rows * top, bound, slope, True), load_shares(count, rows * top, bound, slope, False)
    places = jnp.arange(count)

    def named(sizes, turn):
        used = int((sizes > 0).sum())
        fixed = max(1, used // 4)
        shifted = fixed + (places - fixed + turn * (used - fixed)) % max(1, count - fixed)
        return jnp.zeros((count,), jnp.int32).at[ranking[jnp.where(places < fixed, places, shifted)]].set(jnp.asarray(sizes, jnp.int32))

    sizes = jnp.where(number % 4 == 0, named(heavy_load, number // 4), named(usual, number - number // 4 - 1))
    mixed = jax.random.permutation(jax.random.fold_in(own, 3), count)
    giver, receiver = mixed[0:count // 2 * 2:2], mixed[1:count // 2 * 2:2]
    margin = jnp.minimum(sizes[giver] - 1, bound - sizes[receiver]) // 2
    margin = jnp.where((giver == ranking[0]) | (receiver == ranking[0]) | (sizes[receiver] == 0), 0, jnp.maximum(margin, 0))
    shifted = jax.random.randint(jax.random.fold_in(own, 4), (count // 2,), 0, 1 << 20) % (margin + 1)
    sizes = sizes.at[giver].add(-shifted).at[receiver].add(shifted)
    items = jnp.searchsorted(jnp.cumsum(sizes), jnp.arange(rows * top), side="right").astype(jnp.int32)
    grid = items.reshape(top, rows).T
    grid = grid[jax.random.permutation(jax.random.fold_in(own, 1), rows)]
    turn = jax.random.randint(jax.random.fold_in(own, 2), (rows, 1), 0, top)
    return jnp.take_along_axis(grid, (jnp.arange(top)[None, :] + turn) % top, axis=1)


def load_shares(amount, total, reach, slope, full):
    loads = [(1 << 20) // math.isqrt(standing ** slope) + 1 for standing in range(1, amount + 1)]
    largest = reach if full else min(reach, max(-(-total // amount), total * loads[0] // sum(loads)))
    least = 1 if total - largest >= amount - 1 else 0
    given, rest = [largest] + [least] * (amount - 1), total - largest - least * (amount - 1)
    while rest > 0:
        movable = [i for i in range(1, amount) if given[i] < largest] or [i for i in range(1, amount) if given[i] < reach]
        whole, budget = sum([loads[i] for i in movable]), rest
        for i in movable:
            more = min(reach - given[i], max(1, budget * loads[i] // whole), rest)
            given[i] = given[i] + more
            rest = rest - more
    return np.array(given)


def noise(rng, shape, spread, bound, kind=jnp.bfloat16):
    drawn = jax.random.normal(rng, shape, jnp.float32) * spread
    return jnp.minimum(jnp.maximum(drawn, -bound), bound).astype(kind)


def setup_inputs(seed: int = 0, part: int = 0) -> dict:
    key_list = jax.random.split(jax.random.key(seed), 8)
    part_splits = jax.random.split(jax.random.fold_in(key_list[7], part), 8)
    activations = draw_activations(jax.random.fold_in(jax.random.fold_in(key_list[7], part), 71), part)
    frame_clip = draw_frame_clip(jax.random.fold_in(jax.random.fold_in(key_list[7], part), 71), part)
    conv_weight = noise(key_list[2], (3, 3, 3, CHANNELS, CHANNELS), (27 * CHANNELS) ** -0.5, 0.109375)
    norm_gain = jnp.clip(1.0 + 0.15 * jax.random.normal(key_list[3], (CHANNELS,), jnp.float32), 0.25, 1.75)
    norm_bias = noise(key_list[4], (CHANNELS,), 0.5, 3.0, jnp.float32)
    out_weight = noise(key_list[5], (2, 2, CHANNELS, MOMENTS), (4 * CHANNELS) ** -0.5, 0.25)
    owner_keys = jax.random.split(jax.random.fold_in(part_splits[6], 1), N_SPACE * (FRAMES * HALF_ROWS) // SEND_ROWS)
    owner_turns = jax.random.permutation(jax.random.fold_in(part_splits[6], 3), N_SPACE * (FRAMES * HALF_ROWS) // SEND_ROWS)
    owner = jax.vmap(lambda own, number: shared_out(jax.random.fold_in(part_splits[6], 2), own, number, SEND_ROWS, N_TM, 1, CAPACITY, 2))(owner_keys, owner_turns).reshape((N_SPACE, FRAMES * HALF_ROWS, 1))
    return dict(activations=activations, frame_clip=frame_clip, conv_weight=conv_weight, norm_gain=norm_gain, norm_bias=norm_bias, out_weight=out_weight, owner=owner)


def tap_list(clip_ids):
    frame_total = clip_ids.shape[0]
    position = jnp.arange(frame_total, dtype=jnp.int32)
    padded_ids = jnp.concatenate([jnp.full((2,), -1, jnp.int32), clip_ids])
    matches = [(padded_ids[m:m + frame_total] == clip_ids).astype(jnp.int32) for m in range(3)]
    result = []
    for k in range(3):
        number = matches[k]
        for m in range(k + 1, 3):
            number = number + matches[m]
        result.append(position + 1 - number)
    return result

def plane_conv(frames, kernel):
    return lax.conv_general_dilated(frames, kernel, (1, 1), ((1, 1), (1, 1)), dimension_numbers=('CNHW', 'HWIO', 'CNHW'), precision=lax.Precision.HIGHEST)

def reference(activations, frame_clip, conv_weight, norm_gain, norm_bias, out_weight, owner):
    source = activations.astype(jnp.float32)
    kernels = conv_weight.astype(jnp.float32)
    conv = jnp.zeros(activations.shape, jnp.float32)
    for k, tap_index in enumerate(tap_list(frame_clip)):
        conv = conv + plane_conv(jnp.take(source, tap_index, axis=1), kernels[k])
    conv = conv.astype(jnp.bfloat16).astype(jnp.float32)
    group_size = CHANNELS // GROUPS
    onehot = (frame_clip[:, None] == jnp.arange(CLIPS, dtype=jnp.int32)[None, :]).astype(jnp.float32)
    sums_one = lax.optimization_barrier(jnp.sum(conv, axis=(2, 3))).reshape(GROUPS, group_size, FRAMES).sum(1)
    sums_two = lax.optimization_barrier(jnp.sum(conv * conv, axis=(2, 3))).reshape(GROUPS, group_size, FRAMES).sum(1)
    sums_one = jnp.dot(sums_one, onehot, precision=lax.Precision.HIGHEST)
    sums_two = jnp.dot(sums_two, onehot, precision=lax.Precision.HIGHEST)
    counts = lax.optimization_barrier(jnp.sum(onehot, axis=0)) * (HEIGHT * COLUMNS * group_size)
    mean = sums_one / counts
    rstd = lax.rsqrt(sums_two / counts - mean * mean + 1e-06)
    mean_frame = jnp.repeat(jnp.dot(mean, onehot.T, precision=lax.Precision.HIGHEST), group_size, axis=0)
    rstd_frame = jnp.repeat(jnp.dot(rstd, onehot.T, precision=lax.Precision.HIGHEST), group_size, axis=0)
    scaled = (conv - mean_frame[:, :, None, None]) * rstd_frame[:, :, None, None]
    normed = jax.nn.silu(scaled * norm_gain[:, None, None, None] + norm_bias[:, None, None, None]).astype(jnp.bfloat16)
    patches = normed.astype(jnp.float32).reshape(CHANNELS, FRAMES, HEIGHT // 2, 2, HALF_COLS, 2)
    latent = jnp.einsum('cfrizj,ijco->ofrz', patches, out_weight.astype(jnp.float32), precision=lax.Precision.HIGHEST).astype(jnp.bfloat16)
    row_block = latent.reshape(MOMENTS, FRAMES, N_SPACE, HALF_ROWS, HALF_COLS)
    row_block = row_block.transpose(2, 1, 3, 0, 4).reshape(N_SPACE, FRAMES * HALF_ROWS, MOMENTS, HALF_COLS)
    blocks = owner[:, :, 0].reshape(N_SPACE, N_TM, SEND_ROWS)
    earlier = jnp.arange(SEND_ROWS)[None, :] < jnp.arange(SEND_ROWS)[:, None]
    equal = blocks[:, :, :, None] == blocks[:, :, None, :]
    order_rank = lax.optimization_barrier(jnp.sum((equal & earlier[None, None]).astype(jnp.int32), axis=3))
    target = blocks * (N_TM * CAPACITY) + jnp.arange(N_TM, dtype=jnp.int32)[None, :, None] * CAPACITY + order_rank
    target = target.reshape(N_SPACE, FRAMES * HALF_ROWS)
    owned = jnp.zeros((N_SPACE, N_TM * N_TM * CAPACITY, MOMENTS, HALF_COLS), jnp.bfloat16)
    owned = owned.at[jnp.arange(N_SPACE)[:, None], target].set(row_block)
    return owned
```

```python
import functools

import jax
import jax.numpy as jnp
from jax import lax
from jax.experimental import pallas as pl
from jax.experimental.pallas import tpu as pltpu
from jax.sharding import PartitionSpec as P

CHANNELS = 128
GROUPS = 32
GROUP_SIZE = CHANNELS // GROUPS
F32 = jnp.float32
BF16 = jnp.bfloat16
MESH = pl.DeviceIdType.MESH


def kernel(
    sizes, act, meta_in, weight, gain, bias, out_weight, out,
    x, wt, conv, stat, stats, latent, arrived, meta, ids, sums,
    near_send, near_recv, zrow_send, zrow_recv, meta_send, meta_recv, stat_send, stat_recv,
    lat_send, lat_recv, extra_send, extra_recv, local_sem,
):
    n_tm, n_space, capacity, chunks = sizes
    frames_here, rows, half, columns = act.shape
    lanes = columns // 2
    total = n_tm * n_space * 2
    n_frames = n_tm * frames_here
    lat_rows = rows // 2
    step_rows = rows // chunks
    t = lax.axis_index("tm")
    s = lax.axis_index("space")
    c = lax.axis_index("chan")
    me = (t * n_space + s) * 2 + c
    first = jnp.logical_and(t == 0, c == 1)
    has_main = jnp.logical_or(c == 1, t < n_tm - 1)

    def where_is(flat):
        return {"tm": flat // (2 * n_space), "space": (flat // 2) % n_space, "chan": flat % 2}

    barrier = pltpu.get_barrier_semaphore()

    @pl.loop(1, total)
    def _(step):
        pl.semaphore_signal(
            barrier, inc=1, device_id=where_is(lax.rem(me + step, total)), device_id_type=MESH
        )

    pl.semaphore_wait(barrier, total - 1)

    def remote(src, dst, send, recv, device):
        return pltpu.make_async_remote_copy(
            src_ref=src, dst_ref=dst, send_sem=send, recv_sem=recv, device_id=device,
            device_id_type=MESH,
        )

    def meta_copy(target):
        return remote(
            meta_in, meta.at[t], meta_send.at[target], meta_recv.at[t],
            {"tm": target, "space": s, "chan": c},
        )

    @pl.loop(1, n_tm)
    def _(step):
        meta_copy(lax.rem(t + step, n_tm)).start()

    up_ok, down_ok = t < n_tm - 1, t > 0
    t_up, t_down = jnp.minimum(t + 1, n_tm - 1), jnp.maximum(t - 1, 0)

    def zrow(up, piece):
        frame, slot, core, tt = (1, 0, 1, t_up) if up else (0, 2, 0, t_down)
        return remote(
            act.at[frame, pl.ds(piece * step_rows, step_rows)],
            x.at[slot, pl.ds(1 + piece * step_rows, step_rows), c],
            zrow_send.at[int(up), piece], zrow_recv.at[c, piece],
            {"tm": tt, "space": s, "chan": core},
        )

    def space_of(low):
        return jnp.maximum(s - 1, 0) if low else jnp.minimum(s + 1, n_space - 1)

    def edge(low, core):
        return remote(
            act.at[:, 0 if low else rows - 1],
            x.at[pl.ds(core, 2), rows + 1 if low else 0, c],
            near_send.at[int(low) * 2 + core], near_recv.at[int(low) * 2 + c],
            {"tm": t, "space": space_of(low), "chan": core},
        )

    def zedge(up, low):
        frame, slot, core, tt = (1, 0, 1, t_up) if up else (0, 2, 0, t_down)
        return remote(
            act.at[frame, 0 if low else rows - 1],
            x.at[slot, rows + 1 if low else 0, c],
            near_send.at[4 + int(low) * 2 + int(up)], near_recv.at[4 + int(low) * 2 + c],
            {"tm": tt, "space": space_of(low), "chan": core},
        )

    peer = remote(
        act, x.at[pl.ds(1 - c, 2), pl.ds(1, rows), c], near_send.at[8], near_recv.at[8],
        {"tm": t, "space": s, "chan": 1 - c},
    )
    low_ok, high_ok = s > 0, s < n_space - 1
    sides = ((True, low_ok), (False, high_ok))
    zs = ((True, up_ok), (False, down_ok))

    peer.start()
    for low, ok in sides:
        for up, z_ok in zs:
            @pl.when(jnp.logical_and(ok, z_ok))
            def _(low=low, up=up):
                zedge(up, low).start()
    for piece in range(chunks):
        for up, z_ok in zs:
            @pl.when(z_ok)
            def _(piece=piece, up=up):
                zrow(up, piece).start()
    for low, ok in sides:
        @pl.when(ok)
        def _(low=low):
            edge(low, 0).start()
            edge(low, 1).start()

    meta[t] = meta_in[...]
    for f in range(2):
        x[c + f, pl.ds(1, rows), c] = act[f]
    zero_row = jnp.zeros((3, 2, half, columns), BF16)

    @pl.when(s == 0)
    def _():
        x[:, 0] = zero_row

    @pl.when(s == n_space - 1)
    def _():
        x[:, rows + 1] = zero_row

    @pl.when(first)
    def _():
        x[0, pl.ds(1, rows)] = jnp.zeros((rows, 2, half, columns), BF16)

        @pl.when(s > 0)
        def _():
            x[0, 0] = zero_row[0]

        @pl.when(s < n_space - 1)
        def _():
            x[0, rows + 1] = zero_row[0]

    for k in range(3):
        for i in range(3):
            for j in range(3):
                wt[k, pl.ds(j * 128, 128), pl.ds(i * 128, 128)] = weight[k, i, j].T
    stat[...] = jnp.zeros_like(stat)

    @pl.loop(1, n_tm)
    def _(step):
        source = lax.rem(t + step, n_tm)
        remote(
            meta_in, meta.at[source], meta_send.at[source], meta_recv.at[source],
            {"tm": source, "space": s, "chan": c},
        ).wait_recv()

    to_scalars = pltpu.make_async_copy(meta, ids, local_sem)
    to_scalars.start()
    to_scalars.wait()

    def clip_of(frame):
        frame = jnp.minimum(frame, n_frames - 1)
        return ids[frame // 2, 0, frame % 2]

    my_frame = 2 * t + 2 - c
    my_clip = clip_of(my_frame)
    older = jnp.logical_and(my_frame >= 2, clip_of(jnp.maximum(my_frame - 2, 0)) == my_clip)
    newer = clip_of(jnp.maximum(my_frame - 1, 0)) == my_clip

    peer.wait_recv()
    for low, ok in ((True, high_ok), (False, low_ok)):
        for core in range(2):
            @pl.when(ok)
            def _(low=low, core=core):
                remote(
                    act.at[:, 0], x.at[pl.ds(c, 2), rows + 1 if low else 0, core],
                    near_send.at[int(low) * 2 + core], near_recv.at[int(low) * 2 + core],
                    {"tm": t, "space": s, "chan": c},
                ).wait_recv()

    lane = lax.broadcasted_iota(jnp.int32, (CHANNELS, columns), 1)

    def conv_row(h, kept, taps):
        acc = None
        for k in range(3):
            term = jnp.dot(wt[k], taps[k](h), preferred_element_type=F32)
            acc = term if acc is None else acc + term
        left = jnp.where(lane == 0, 0.0, pltpu.roll(acc[0:128], 1, 1))
        right = jnp.where(lane == columns - 1, 0.0, pltpu.roll(acc[256:384], columns - 1, 1))
        value = (left + acc[128:256] + right).astype(BF16)
        conv[kept, h] = value
        value = value.astype(F32)
        a, b = value[:, :lanes], value[:, lanes:]
        sums[0] += a + b
        sums[1] += a * a + b * b

    def slab(slot):
        return lambda h: x[slot, pl.ds(h, 3)].reshape(3 * CHANNELS, columns)

    def sums_to(row):
        stat[pl.ds(row, 1), :] = jnp.sum(sums[0].T, axis=0, keepdims=True)
        stat[pl.ds(row + 1, 1), :] = jnp.sum(sums[1].T, axis=0, keepdims=True)

    @pl.when(first)
    def _():
        sums[...] = jnp.zeros_like(sums)

        @pl.loop(0, rows)
        def _(h):
            conv_row(h, 1, [slab(1)] * 3)

        sums_to(2)

    gets_z = jnp.logical_or(jnp.logical_and(c == 1, down_ok), jnp.logical_and(c == 0, up_ok))
    z_slot = 2 * (1 - c)

    def wait_zedge(low, ok):
        for core in range(2):
            @pl.when(jnp.logical_and(gets_z, ok))
            def _(core=core):
                remote(
                    act.at[0, 0], x.at[z_slot, rows + 1 if low else 0, core],
                    near_send.at[4 + int(low) * 2], near_recv.at[4 + int(low) * 2 + core],
                    {"tm": t, "space": s, "chan": c},
                ).wait_recv()

    def wait_zrow(piece):
        for core in range(2):
            @pl.when(gets_z)
            def _(core=core):
                remote(
                    act.at[0, pl.ds(piece * step_rows, step_rows)],
                    x.at[z_slot, pl.ds(1 + piece * step_rows, step_rows), core],
                    zrow_send.at[0, piece], zrow_recv.at[core, piece],
                    {"tm": t, "space": s, "chan": c},
                ).wait_recv()

    def tap_old(h):
        return jnp.where(older, slab(0)(h), tap_mid(h))

    def tap_mid(h):
        return jnp.where(newer, slab(1)(h), slab(2)(h))

    taps = [tap_old, tap_mid, slab(2)]
    wait_zedge(False, low_ok)
    wait_zedge(True, high_ok)

    @pl.when(has_main)
    def _():
        sums[...] = jnp.zeros_like(sums)

    for piece in range(chunks):
        wait_zrow(piece)
        begin = 0 if piece == 0 else piece * step_rows - 1
        end = rows if piece == chunks - 1 else (piece + 1) * step_rows - 1

        @pl.when(has_main)
        def _(begin=begin, end=end):
            @pl.loop(begin, end)
            def _(h):
                conv_row(h, 0, taps)

    @pl.when(has_main)
    def _():
        sums_to(0)

    def stat_copy(target):
        return remote(
            stat, stats.at[me], stat_send.at[target], stat_recv.at[me], where_is(target)
        )

    stats[me] = stat[...]

    @pl.loop(1, total)
    def _(step):
        stat_copy(lax.rem(me + step, total)).start()

    gain_c = jnp.broadcast_to(gain[...], (128, 128)).T
    bias_c = jnp.broadcast_to(bias[...], (128, 128)).T
    spread_row = lax.broadcasted_iota(jnp.int32, (columns, columns), 0)
    spread_col = lax.broadcasted_iota(jnp.int32, (columns, columns), 1)
    picked = jnp.where(spread_col < lanes, 2 * spread_col, 2 * (spread_col - lanes) + 1)
    spread = jnp.where(spread_row == picked, 1.0, 0.0).astype(BF16)

    @pl.loop(1, total)
    def _(step):
        source = lax.rem(me + step, total)
        remote(
            stat, stats.at[source], stat_send.at[source], stat_recv.at[source], where_is(source)
        ).wait_recv()

    lane8 = lax.broadcasted_iota(jnp.int32, (8, 128), 1)

    def group_sum(v):
        v = v + jnp.where(lane8 % 2 == 0, pltpu.roll(v, 127, 1), pltpu.roll(v, 1, 1))
        return v + jnp.where(lane8 % 4 < 2, pltpu.roll(v, 126, 1), pltpu.roll(v, 2, 1))

    def finish(kept, clip):
        def add_main(source, carry):
            frame = 2 * (source // (2 * n_space)) + 2 - source % 2
            same = jnp.logical_and(frame < n_frames, clip_of(frame) == clip)
            return carry + jnp.where(same, stats[source], 0.0)

        gathered = lax.fori_loop(0, total, add_main, jnp.zeros((8, 128), F32))
        zero_frame = jnp.zeros((8, 128), F32)
        for space in range(n_space):
            zero_frame += stats[2 * space + 1]
        zero_frame = jnp.where(clip_of(0) == clip, zero_frame, 0.0)
        number = jnp.float32(0)
        for frame in range(n_frames):
            number += jnp.where(clip_of(frame) == clip, 1.0, 0.0)
        count = number * float(rows * n_space * columns * GROUP_SIZE)
        gathered = group_sum(gathered)
        zero_frame = group_sum(zero_frame)
        count = jnp.broadcast_to(count, (1, 128))
        mean = (gathered[0:1] + zero_frame[2:3]) / count
        var = (gathered[1:2] + zero_frame[3:4]) / count - mean * mean
        rstd = lax.rsqrt(var + 1e-6)
        mean_c = jnp.broadcast_to(mean, (128, 128)).T
        scale_c = jnp.broadcast_to(rstd, (128, 128)).T * gain_c

        @pl.loop(0, lat_rows)
        def _(r):
            parts = []
            for i in range(2):
                value = conv[kept, 2 * r + i].astype(F32)
                pieces = []
                for u in range(2):
                    v = (value[:, u * lanes:(u + 1) * lanes] - mean_c) * scale_c + bias_c
                    pieces.append((v / (1.0 + jnp.exp(-v))).astype(BF16))
                normed = jnp.concatenate(pieces, axis=1)
                sorted_ = jnp.dot(normed, spread, preferred_element_type=F32).astype(BF16)
                parts += [sorted_[:, :lanes], sorted_[:, lanes:]]
            stacked = jnp.concatenate(parts, axis=0)
            result = lax.dot_general(
                out_weight[...], stacked, (((0,), (0,)), ((), ())), preferred_element_type=F32
            ).astype(BF16)
            latent[kept, 0, r] = result[0:16]
            latent[kept, 1, r] = result[16:32]

    def lat_copy(kept, frame, target, core, send, recv):
        return remote(
            latent.at[kept, core], arrived.at[frame], send.at[target * 2 + core], recv,
            {"tm": target, "space": s, "chan": core},
        )

    here = t * 2 + c
    places = n_tm * 2

    def send_latent(kept, frame, send, recv):
        arrived[frame] = latent[kept, c]

        @pl.loop(1, places)
        def _(step):
            target = lax.rem(here + step, places)
            lat_copy(kept, frame, target // 2, target % 2, send, recv).start()

    @pl.when(first)
    def _():
        finish(1, clip_of(0))
        send_latent(1, 0, extra_send, extra_recv)

    @pl.when(has_main)
    def _():
        finish(0, my_clip)
        send_latent(0, my_frame, lat_send, lat_recv.at[my_frame])

    @pl.loop(1, n_frames)
    def _(frame):
        @pl.when(frame != my_frame)
        def _():
            lat_copy(0, frame, t, c, lat_send, lat_recv.at[frame]).wait_recv()

    @pl.when(jnp.logical_not(first))
    def _():
        lat_copy(0, 0, t, c, lat_send, extra_recv).wait_recv()

    @pl.loop(0, n_tm)
    def _(b):
        taken = jnp.int32(0)
        slots = []
        for n in range(2 * lat_rows):
            hit = ids[b, 0, frames_here + n] == t
            slots.append(jnp.where(hit, taken, -1))
            taken = taken + jnp.where(hit, 1, 0)
        for j in range(capacity):
            value = jnp.zeros((16, lanes), BF16)
            for n in range(2 * lat_rows):
                row = arrived[2 * b + n // lat_rows, n % lat_rows]
                value = jnp.where(slots[n] == j, row, value)
            out[0, b * capacity + j] = value

    @pl.loop(1, n_tm)
    def _(step):
        meta_copy(lax.rem(t + step, n_tm)).wait_send()

    peer.wait_send()
    for low, ok in sides:
        for up, z_ok in zs:
            @pl.when(jnp.logical_and(ok, z_ok))
            def _(low=low, up=up):
                zedge(up, low).wait_send()

        @pl.when(ok)
        def _(low=low):
            edge(low, 0).wait_send()
            edge(low, 1).wait_send()
    for piece in range(chunks):
        for up, z_ok in zs:
            @pl.when(z_ok)
            def _(piece=piece, up=up):
                zrow(up, piece).wait_send()

    @pl.loop(1, total)
    def _(step):
        stat_copy(lax.rem(me + step, total)).wait_send()

    def latents_left(kept, frame, send, recv):
        @pl.loop(1, places)
        def _(step):
            target = lax.rem(here + step, places)
            lat_copy(kept, frame, target // 2, target % 2, send, recv).wait_send()

    @pl.when(first)
    def _():
        latents_left(1, 0, extra_send, extra_recv)

    @pl.when(has_main)
    def _():
        latents_left(0, my_frame, lat_send, lat_recv.at[my_frame])


def solution(mesh):
    n_tm, n_space = mesh.shape["tm"], mesh.shape["space"]
    total = n_tm * n_space * 2

    def shards(activations, frame_clip, conv_weight, norm_gain, norm_bias, out_weight, owner):
        half, frames_here, rows, columns = activations.shape
        lat_rows = rows // 2
        capacity = max(2, 2 * frames_here * lat_rows // n_tm)
        chunks = 4
        act = activations.transpose(1, 2, 0, 3)
        numbers = jnp.concatenate([frame_clip, owner.reshape(-1)])
        meta = jnp.zeros((8, 128), jnp.int32).at[0, : numbers.shape[0]].set(numbers)
        moments = out_weight.shape[-1]
        dma = pltpu.SemaphoreType.DMA
        return pl.pallas_call(
            functools.partial(kernel, (n_tm, n_space, capacity, chunks)),
            out_shape=jax.ShapeDtypeStruct(
                (1, n_tm * capacity, moments // 2, columns // 2), BF16
            ),
            in_specs=[pl.BlockSpec(memory_space=pltpu.VMEM)] * 6,
            out_specs=pl.BlockSpec(memory_space=pltpu.VMEM),
            scratch_shapes=[
                pltpu.VMEM((3, rows + 2, 2, half, columns), BF16),
                pltpu.VMEM((3, 384, 384), BF16),
                pltpu.VMEM((2, rows, CHANNELS, columns), BF16),
                pltpu.VMEM((8, 128), F32),
                pltpu.VMEM((total, 8, 128), F32),
                pltpu.VMEM((2, 2, lat_rows, moments // 2, columns // 2), BF16),
                pltpu.VMEM((n_tm * frames_here, lat_rows, moments // 2, columns // 2), BF16),
                pltpu.VMEM((n_tm, 8, 128), jnp.int32),
                pltpu.SMEM((n_tm, 8, 128), jnp.int32),
                pltpu.VMEM((2, CHANNELS, columns // 2), F32),
                dma((9,)),
                dma((9,)),
                dma((2, chunks)),
                dma((2, chunks)),
                dma((n_tm,)),
                dma((n_tm,)),
                dma((total,)),
                dma((total,)),
                dma((2 * n_tm,)),
                dma((n_tm * frames_here,)),
                dma((2 * n_tm,)),
                dma(()),
                dma(()),
            ],
            compiler_params=pltpu.CompilerParams(
                collective_id=0, has_side_effects=True, vmem_limit_bytes=48 << 20
            ),
        )(
            act, meta, conv_weight, norm_gain.reshape(1, -1), norm_bias.reshape(1, -1),
            out_weight.reshape(-1, moments),
        )

    placed = (
        P(("groups", "chan"), "tm", "space", None),
        P(("groups", "tm")),
        P(),
        P(),
        P(),
        P(),
        P(("groups", "space"), "tm", None),
    )
    return jax.shard_map(
        shards,
        mesh=mesh,
        in_specs=placed,
        out_specs=P(("groups", "space"), "tm", "chan", None),
        check_vma=False,
    )
```

```python
import functools

import jax
import jax.numpy as jnp
from jax import lax
from jax.experimental import pallas as pl
from jax.experimental.pallas import tpu as pltpu
from jax.sharding import PartitionSpec as P

CHANNELS = 128
GROUPS = 32
GROUP_SIZE = CHANNELS // GROUPS
F32 = jnp.float32
BF16 = jnp.bfloat16
MESH = pl.DeviceIdType.MESH


def kernel(
    sizes, clip_hbm, owner_hbm, act_in, weight_in, gain_in, bias_in, out_weight_in, out,
    clip_in, owner_in, act_raw, act, weight, gain, bias, out_weight, meta_in,
    x, wt, conv, stat, stats, latent, arrived, meta, ids, sums,
    near_send, near_recv, zrow_send, zrow_recv, meta_send, meta_recv, stat_send, stat_recv,
    lat_send, lat_recv, extra_send, extra_recv, local_sem,
):
    n_tm, n_space, capacity, chunks = sizes
    frames_here, rows, half, columns = act.shape
    lanes = columns // 2
    total = n_tm * n_space * 2
    n_frames = n_tm * frames_here
    lat_rows = rows // 2
    step_rows = rows // chunks
    t = lax.axis_index("tm")
    s = lax.axis_index("space")
    c = lax.axis_index("chan")
    me = (t * n_space + s) * 2 + c
    first = t == 0
    piece_rows = lat_rows // 2
    reach = n_tm // 2
    has_main = jnp.logical_or(c == 1, t < n_tm - 1)

    def where_is(flat):
        return {"tm": flat // (2 * n_space), "space": (flat // 2) % n_space, "chan": flat % 2}

    fetches = [
        pltpu.make_async_copy(source, held, local_sem.at[1 + n])
        for n, (source, held) in enumerate((
            (act_in, act_raw), (weight_in, weight), (gain_in, gain), (bias_in, bias),
            (out_weight_in, out_weight),
            (clip_hbm, clip_in), (owner_hbm, owner_in),
        ))
    ]
    for fetch in fetches:
        fetch.start()
    stats[...] = jnp.zeros_like(stats)
    stat[...] = jnp.zeros_like(stat)

    barrier = pltpu.get_barrier_semaphore()

    @pl.loop(1, total)
    def _(step):
        pl.semaphore_signal(
            barrier, inc=1, device_id=where_is(lax.rem(me + step, total)), device_id_type=MESH
        )

    fetches[5].wait()
    fetches[6].wait()
    place = lax.broadcasted_iota(jnp.int32, (8, 128), 1)
    numbers = jnp.zeros((8, 128), jnp.int32)
    for n in range(frames_here):
        numbers = jnp.where(place == n, clip_in[0, n], numbers)
    for n in range(frames_here * lat_rows):
        numbers = jnp.where(place == frames_here + n, owner_in[0, n], numbers)
    meta_in[...] = numbers
    meta[t] = numbers
    fetches[0].wait()
    for f in range(frames_here):
        turned = jnp.transpose(act_raw[:, f], (1, 0, 2))
        act[f] = turned
        x[c + f, pl.ds(1, rows), c] = turned

    pl.semaphore_wait(barrier, total - 1)

    def remote(src, dst, send, recv, device):
        return pltpu.make_async_remote_copy(
            src_ref=src, dst_ref=dst, send_sem=send, recv_sem=recv, device_id=device,
            device_id_type=MESH,
        )

    def meta_copy(target):
        return remote(
            meta_in, meta.at[t], meta_send.at[target], meta_recv.at[t],
            {"tm": target, "space": s, "chan": c},
        )

    @pl.loop(1, n_tm)
    def _(step):
        meta_copy(lax.rem(t + step, n_tm)).start()

    up_ok, down_ok = t < n_tm - 1, t > 0
    t_up, t_down = jnp.minimum(t + 1, n_tm - 1), jnp.maximum(t - 1, 0)

    def zrow(up, piece):
        frame, slot, core, tt = (1, 0, 1, t_up) if up else (0, 2, 0, t_down)
        return remote(
            act.at[frame, pl.ds(piece * step_rows, step_rows)],
            x.at[slot, pl.ds(1 + piece * step_rows, step_rows), c],
            zrow_send.at[int(up), piece], zrow_recv.at[c, piece],
            {"tm": tt, "space": s, "chan": core},
        )

    def space_of(low):
        return jnp.maximum(s - 1, 0) if low else jnp.minimum(s + 1, n_space - 1)

    def edge(low, core):
        return remote(
            act.at[:, 0 if low else rows - 1],
            x.at[pl.ds(core, 2), rows + 1 if low else 0, c],
            near_send.at[int(low) * 2 + core], near_recv.at[int(low) * 2 + c],
            {"tm": t, "space": space_of(low), "chan": core},
        )

    def zedge(up, low):
        frame, slot, core, tt = (1, 0, 1, t_up) if up else (0, 2, 0, t_down)
        return remote(
            act.at[frame, 0 if low else rows - 1],
            x.at[slot, rows + 1 if low else 0, c],
            near_send.at[4 + int(low) * 2 + int(up)], near_recv.at[4 + int(low) * 2 + c],
            {"tm": tt, "space": space_of(low), "chan": core},
        )

    peer = remote(
        act, x.at[pl.ds(1 - c, 2), pl.ds(1, rows), c], near_send.at[8], near_recv.at[8],
        {"tm": t, "space": s, "chan": 1 - c},
    )
    low_ok, high_ok = s > 0, s < n_space - 1
    sides = ((True, low_ok), (False, high_ok))
    zs = ((True, up_ok), (False, down_ok))

    peer.start()
    for low, ok in sides:
        for up, z_ok in zs:
            @pl.when(jnp.logical_and(ok, z_ok))
            def _(low=low, up=up):
                zedge(up, low).start()
    for piece in range(chunks):
        for up, z_ok in zs:
            @pl.when(z_ok)
            def _(piece=piece, up=up):
                zrow(up, piece).start()
    for low, ok in sides:
        @pl.when(ok)
        def _(low=low):
            edge(low, 0).start()
            edge(low, 1).start()

    zero_row = jnp.zeros((3, 2, half, columns), BF16)

    @pl.when(s == 0)
    def _():
        x[:, 0] = zero_row

    @pl.when(s == n_space - 1)
    def _():
        x[:, rows + 1] = zero_row

    @pl.when(jnp.logical_and(first, c == 1))
    def _():
        x[0, pl.ds(1, rows)] = jnp.zeros((rows, 2, half, columns), BF16)

        @pl.when(s > 0)
        def _():
            x[0, 0] = zero_row[0]

        @pl.when(s < n_space - 1)
        def _():
            x[0, rows + 1] = zero_row[0]

    for fetch in fetches[1:5]:
        fetch.wait()
    for k in range(3):
        for i in range(3):
            for j in range(3):
                wt[k, pl.ds(j * 128, 128), pl.ds(i * 128, 128)] = weight[k, i, j].T
    gain_c = jnp.broadcast_to(gain[...], (128, 128)).T
    bias_c = jnp.broadcast_to(bias[...], (128, 128)).T * 0.5

    @pl.loop(1, n_tm)
    def _(step):
        source = lax.rem(t + step, n_tm)
        remote(
            meta_in, meta.at[source], meta_send.at[source], meta_recv.at[source],
            {"tm": source, "space": s, "chan": c},
        ).wait_recv()

    to_scalars = pltpu.make_async_copy(meta, ids, local_sem.at[0])
    to_scalars.start()
    to_scalars.wait()

    def clip_of(frame):
        frame = jnp.minimum(frame, n_frames - 1)
        return ids[frame // 2, 0, frame % 2]

    my_frame = 2 * t + 2 - c
    my_clip = clip_of(my_frame)
    older = jnp.logical_and(my_frame >= 2, clip_of(jnp.maximum(my_frame - 2, 0)) == my_clip)
    newer = clip_of(jnp.maximum(my_frame - 1, 0)) == my_clip

    peer.wait_recv()
    for low, ok in ((True, high_ok), (False, low_ok)):
        for core in range(2):
            @pl.when(ok)
            def _(low=low, core=core):
                remote(
                    act.at[:, 0], x.at[pl.ds(c, 2), rows + 1 if low else 0, core],
                    near_send.at[int(low) * 2 + core], near_recv.at[int(low) * 2 + core],
                    {"tm": t, "space": s, "chan": c},
                ).wait_recv()

    lane = lax.broadcasted_iota(jnp.int32, (CHANNELS, columns), 1)

    def conv_row(h, kept, taps):
        acc = None
        for k in range(3):
            term = jnp.dot(wt[k], taps[k](h), preferred_element_type=F32)
            acc = term if acc is None else acc + term
        left = jnp.where(lane == 0, 0.0, pltpu.roll(acc[0:128], 1, 1))
        right = jnp.where(lane == columns - 1, 0.0, pltpu.roll(acc[256:384], columns - 1, 1))
        value = (left + acc[128:256] + right).astype(BF16)
        conv[kept, h] = value
        value = value.astype(F32)
        a, b = value[:, :lanes], value[:, lanes:]
        sums[0] += a + b
        sums[1] += a * a + b * b

    def slab(slot):
        return lambda h: x[slot, pl.ds(h, 3)].reshape(3 * CHANNELS, columns)

    def sums_to(row):
        stat[pl.ds(row, 1), :] = jnp.sum(sums[0].T, axis=0, keepdims=True)
        stat[pl.ds(row + 1, 1), :] = jnp.sum(sums[1].T, axis=0, keepdims=True)

    @pl.when(first)
    def _():
        sums[...] = jnp.zeros_like(sums)

        @pl.loop(c * (rows // 2), (c + 1) * (rows // 2))
        def _(h):
            conv_row(h, 1, [slab(c)] * 3)

        sums_to(2)

    gets_z = jnp.logical_or(jnp.logical_and(c == 1, down_ok), jnp.logical_and(c == 0, up_ok))
    z_slot = 2 * (1 - c)

    def wait_zedge(low, ok):
        for core in range(2):
            @pl.when(jnp.logical_and(gets_z, ok))
            def _(core=core):
                remote(
                    act.at[0, 0], x.at[z_slot, rows + 1 if low else 0, core],
                    near_send.at[4 + int(low) * 2], near_recv.at[4 + int(low) * 2 + core],
                    {"tm": t, "space": s, "chan": c},
                ).wait_recv()

    def wait_zrow(piece):
        for core in range(2):
            @pl.when(gets_z)
            def _(core=core):
                remote(
                    act.at[0, pl.ds(piece * step_rows, step_rows)],
                    x.at[z_slot, pl.ds(1 + piece * step_rows, step_rows), core],
                    zrow_send.at[0, piece], zrow_recv.at[core, piece],
                    {"tm": t, "space": s, "chan": c},
                ).wait_recv()

    def tap_old(h):
        return jnp.where(older, slab(0)(h), tap_mid(h))

    def tap_mid(h):
        return jnp.where(newer, slab(1)(h), slab(2)(h))

    taps = [tap_old, tap_mid, slab(2)]
    wait_zedge(False, low_ok)
    wait_zedge(True, high_ok)

    @pl.when(has_main)
    def _():
        sums[...] = jnp.zeros_like(sums)

    for piece in range(chunks):
        wait_zrow(piece)
        begin = 0 if piece == 0 else piece * step_rows - 1
        end = rows if piece == chunks - 1 else (piece + 1) * step_rows - 1

        @pl.when(has_main)
        def _(begin=begin, end=end):
            @pl.loop(begin, end)
            def _(h):
                conv_row(h, 0, taps)

    @pl.when(has_main)
    def _():
        sums_to(0)

    def stat_copy(target):
        return remote(
            stat, stats.at[me], stat_send.at[target], stat_recv.at[me], where_is(target)
        )

    stats[me] = stat[...]

    def near(device):
        return jnp.abs(device // (2 * n_space) - t) <= reach

    @pl.loop(1, total)
    def _(step):
        target = lax.rem(me + step, total)

        @pl.when(near(target))
        def _():
            stat_copy(target).start()

    spread_row = lax.broadcasted_iota(jnp.int32, (columns, columns), 0)
    spread_col = lax.broadcasted_iota(jnp.int32, (columns, columns), 1)
    picked = jnp.where(spread_col < lanes, 2 * spread_col, 2 * (spread_col - lanes) + 1)
    spread = jnp.where(spread_row == picked, 1.0, 0.0).astype(BF16)

    @pl.loop(1, total)
    def _(step):
        source = lax.rem(me + step, total)

        @pl.when(near(source))
        def _():
            remote(
                stat, stats.at[source], stat_send.at[source], stat_recv.at[source],
                where_is(source),
            ).wait_recv()

    lane8 = lax.broadcasted_iota(jnp.int32, (8, 128), 1)

    def group_sum(v):
        v = v + jnp.where(lane8 % 2 == 0, pltpu.roll(v, 127, 1), pltpu.roll(v, 1, 1))
        return v + jnp.where(lane8 % 4 < 2, pltpu.roll(v, 126, 1), pltpu.roll(v, 2, 1))

    weights = jnp.concatenate([out_weight[q] for q in range(4)], axis=1)

    def moments_of(clip):
        def add_main(source, carry):
            frame = 2 * (source // (2 * n_space)) + 2 - source % 2
            same = jnp.logical_and(frame < n_frames, clip_of(frame) == clip)
            return carry + jnp.where(same, stats[source], 0.0)

        gathered = lax.fori_loop(0, total, add_main, jnp.zeros((8, 128), F32))
        zero_frame = jnp.zeros((8, 128), F32)
        for n in range(2 * n_space):
            zero_frame += stats[n]
        zero_frame = jnp.where(clip_of(0) == clip, zero_frame, 0.0)
        number = jnp.float32(0)
        for frame in range(n_frames):
            number += jnp.where(clip_of(frame) == clip, 1.0, 0.0)
        count = number * float(rows * n_space * columns * GROUP_SIZE)
        gathered = group_sum(gathered)
        zero_frame = group_sum(zero_frame)
        count = jnp.broadcast_to(count, (1, 128))
        mean = (gathered[0:1] + zero_frame[2:3]) / count
        var = (gathered[1:2] + zero_frame[3:4]) / count - mean * mean
        rstd = lax.rsqrt(var + 1e-6)
        mean_c = jnp.broadcast_to(mean, (128, 128)).T
        scale_c = jnp.broadcast_to(rstd, (128, 128)).T * gain_c * 0.5
        return mean_c, scale_c

    def finish(kept, piece, mean_c, scale_c):
        rows_in = []
        for q in range(2 * piece_rows):
            value = conv[kept, 2 * piece_rows * piece + q].astype(F32)
            pieces = []
            for u in range(2):
                v = (value[:, u * lanes:(u + 1) * lanes] - mean_c) * scale_c + bias_c
                pieces.append((v + v * jnp.tanh(v)).astype(BF16))
            rows_in.append(jnp.concatenate(pieces, axis=1))
        sorted_ = jnp.dot(
            jnp.concatenate(rows_in, axis=0), spread, preferred_element_type=F32
        ).astype(BF16)
        wide = jnp.concatenate(
            [
                jnp.concatenate(
                    [
                        sorted_[(2 * r + i) * 128:(2 * r + i + 1) * 128, j * lanes:(j + 1) * lanes]
                        for i in range(2) for j in range(2)
                    ],
                    axis=0,
                )
                for r in range(piece_rows)
            ],
            axis=1,
        )
        result = jnp.dot(weights, wide, preferred_element_type=F32).astype(BF16)
        for r in range(piece_rows):
            latent[kept, 0, piece * piece_rows + r] = result[0:16, r * lanes:(r + 1) * lanes]
            latent[kept, 1, piece * piece_rows + r] = result[16:32, r * lanes:(r + 1) * lanes]

    def lat_copy(kept, piece, frame, target, core, send, recv):
        span = pl.ds(piece * piece_rows, piece_rows)
        return remote(
            latent.at[kept, core, span], arrived.at[frame, span], send.at[target * 2 + core], recv,
            {"tm": target, "space": s, "chan": core},
        )

    here = t * 2 + c
    places = n_tm * 2

    def send_latent(kept, piece, frame, send, recv):
        span = pl.ds(piece * piece_rows, piece_rows)
        arrived[frame, span] = latent[kept, c, span]

        @pl.loop(1, places)
        def _(step):
            target = lax.rem(here + step, places)
            lat_copy(kept, piece, frame, target // 2, target % 2, send, recv).start()

    @pl.when(first)
    def _():
        finish(1, c, *moments_of(clip_of(0)))
        send_latent(1, c, 0, extra_send, extra_recv.at[c])

    @pl.when(has_main)
    def _():
        found = moments_of(my_clip)
        for piece in range(2):
            finish(0, piece, *found)
            send_latent(0, piece, my_frame, lat_send.at[piece], lat_recv.at[my_frame, piece])

    @pl.loop(1, n_frames)
    def _(frame):
        @pl.when(frame != my_frame)
        def _():
            for piece in range(2):
                lat_copy(
                    0, piece, frame, t, c, lat_send.at[piece], lat_recv.at[frame, piece]
                ).wait_recv()

    for piece in range(2):
        @pl.when(jnp.logical_not(jnp.logical_and(first, c == piece)))
        def _(piece=piece):
            lat_copy(0, piece, 0, t, c, lat_send.at[piece], extra_recv.at[piece]).wait_recv()

    @pl.loop(0, n_tm)
    def _(b):
        taken = jnp.int32(0)
        slots = []
        for n in range(2 * lat_rows):
            hit = ids[b, 0, frames_here + n] == t
            slots.append(jnp.where(hit, taken, -1))
            taken = taken + jnp.where(hit, 1, 0)
        for j in range(capacity):
            value = jnp.zeros((16, lanes), BF16)
            for n in range(2 * lat_rows):
                row = arrived[2 * b + n // lat_rows, n % lat_rows]
                value = jnp.where(slots[n] == j, row, value)
            out[0, b * capacity + j] = value

    @pl.loop(1, n_tm)
    def _(step):
        meta_copy(lax.rem(t + step, n_tm)).wait_send()

    peer.wait_send()
    for low, ok in sides:
        for up, z_ok in zs:
            @pl.when(jnp.logical_and(ok, z_ok))
            def _(low=low, up=up):
                zedge(up, low).wait_send()

        @pl.when(ok)
        def _(low=low):
            edge(low, 0).wait_send()
            edge(low, 1).wait_send()
    for piece in range(chunks):
        for up, z_ok in zs:
            @pl.when(z_ok)
            def _(piece=piece, up=up):
                zrow(up, piece).wait_send()

    @pl.loop(1, total)
    def _(step):
        target = lax.rem(me + step, total)

        @pl.when(near(target))
        def _():
            stat_copy(target).wait_send()

    def latents_left(kept, piece, frame, send, recv):
        @pl.loop(1, places)
        def _(step):
            target = lax.rem(here + step, places)
            lat_copy(kept, piece, frame, target // 2, target % 2, send, recv).wait_send()

    @pl.when(first)
    def _():
        latents_left(1, c, 0, extra_send, extra_recv.at[c])

    @pl.when(has_main)
    def _():
        for piece in range(2):
            latents_left(0, piece, my_frame, lat_send.at[piece], lat_recv.at[my_frame, piece])


def solution(mesh):
    n_tm, n_space = mesh.shape["tm"], mesh.shape["space"]
    total = n_tm * n_space * 2

    def shards(activations, frame_clip, conv_weight, norm_gain, norm_bias, out_weight, owner):
        half, frames_here, rows, columns = activations.shape
        lat_rows = rows // 2
        capacity = max(2, 2 * frames_here * lat_rows // n_tm)
        chunks = rows
        moments = out_weight.shape[-1]
        dma = pltpu.SemaphoreType.DMA
        return pl.pallas_call(
            functools.partial(kernel, (n_tm, n_space, capacity, chunks)),
            out_shape=jax.ShapeDtypeStruct(
                (1, n_tm * capacity, moments // 2, columns // 2), BF16
            ),
            in_specs=[pl.BlockSpec(memory_space=pltpu.HBM)] * 7,
            out_specs=pl.BlockSpec(memory_space=pltpu.VMEM),
            scratch_shapes=[
                pltpu.SMEM((1, frames_here), jnp.int32),
                pltpu.SMEM((1, frames_here * lat_rows), jnp.int32),
                pltpu.VMEM(activations.shape, BF16),
                pltpu.VMEM((frames_here, rows, half, columns), BF16),
                pltpu.VMEM(conv_weight.shape, BF16),
                pltpu.VMEM((1, CHANNELS), F32),
                pltpu.VMEM((1, CHANNELS), F32),
                pltpu.VMEM((4, moments, CHANNELS), BF16),
                pltpu.VMEM((8, 128), jnp.int32),
                pltpu.VMEM((3, rows + 2, 2, half, columns), BF16),
                pltpu.VMEM((3, 384, 384), BF16),
                pltpu.VMEM((2, rows, CHANNELS, columns), BF16),
                pltpu.VMEM((8, 128), F32),
                pltpu.VMEM((total, 8, 128), F32),
                pltpu.VMEM((2, 2, lat_rows, moments // 2, columns // 2), BF16),
                pltpu.VMEM((n_tm * frames_here, lat_rows, moments // 2, columns // 2), BF16),
                pltpu.VMEM((n_tm, 8, 128), jnp.int32),
                pltpu.SMEM((n_tm, 8, 128), jnp.int32),
                pltpu.VMEM((2, CHANNELS, columns // 2), F32),
                dma((9,)),
                dma((9,)),
                dma((2, chunks)),
                dma((2, chunks)),
                dma((n_tm,)),
                dma((n_tm,)),
                dma((total,)),
                dma((total,)),
                dma((2, 2 * n_tm)),
                dma((n_tm * frames_here, 2)),
                dma((2 * n_tm,)),
                dma((2,)),
                dma((8,)),
            ],
            compiler_params=pltpu.CompilerParams(
                collective_id=0, has_side_effects=True, vmem_limit_bytes=67_043_328
            ),
        )(
            frame_clip.reshape(1, -1), owner.reshape(1, -1), activations, conv_weight,
            norm_gain.reshape(1, -1), norm_bias.reshape(1, -1),
            out_weight.transpose(0, 1, 3, 2).reshape(4, moments, CHANNELS),
        )

    placed = (
        P(("groups", "chan"), "tm", "space", None),
        P(("groups", "tm")),
        P(),
        P(),
        P(),
        P(),
        P(("groups", "space"), "tm", None),
    )
    return jax.shard_map(
        shards,
        mesh=mesh,
        in_specs=placed,
        out_specs=P(("groups", "space"), "tm", "chan", None),
        check_vma=False,
    )
```

```python
import functools

import jax
import jax.numpy as jnp
from jax import lax
from jax.experimental import pallas as pl
from jax.experimental.pallas import tpu as pltpu
from jax.sharding import PartitionSpec as P

CHANNELS = 128
GROUPS = 32
GROUP_SIZE = CHANNELS // GROUPS
F32 = jnp.float32
BF16 = jnp.bfloat16
MESH = pl.DeviceIdType.MESH


def kernel(
    sizes, clip_hbm, owner_hbm, act_in, weight_in, gain_in, bias_in, out_weight_in, out,
    clip_in, owner_in, act_raw, act, weight, gain, bias, out_weight, meta_in,
    x, wt, conv, stat, stats, latent, arrived, meta, ids, ids_near, sums,
    near_send, near_recv, zrow_send, zrow_recv, meta_send, meta_recv, stat_send, stat_recv,
    lat_send, lat_recv, extra_send, extra_recv, local_sem,
):
    n_tm, n_space, capacity, chunks = sizes
    frames_here, rows, half, columns = act.shape
    lanes = columns // 2
    total = n_tm * n_space * 2
    n_frames = n_tm * frames_here
    lat_rows = rows // 2
    step_rows = rows // chunks
    t = lax.axis_index("tm")
    s = lax.axis_index("space")
    c = lax.axis_index("chan")
    me = (t * n_space + s) * 2 + c
    first = t == 0
    piece_rows = lat_rows // 2
    reach = n_tm // 2
    has_main = jnp.logical_or(c == 1, t < n_tm - 1)

    def where_is(flat):
        return {"tm": flat // (2 * n_space), "space": (flat // 2) % n_space, "chan": flat % 2}

    fetches = [
        pltpu.make_async_copy(source, held, local_sem.at[1 + n])
        for n, (source, held) in enumerate((
            (act_in, act_raw), (weight_in, weight), (gain_in, gain), (bias_in, bias),
            (out_weight_in, out_weight),
            (clip_hbm, clip_in), (owner_hbm, owner_in),
        ))
    ]
    for fetch in fetches:
        fetch.start()
    stats[...] = jnp.zeros_like(stats)
    stat[...] = jnp.zeros_like(stat)

    barrier = pltpu.get_barrier_semaphore()

    @pl.loop(1, total)
    def _(step):
        pl.semaphore_signal(
            barrier, inc=1, device_id=where_is(lax.rem(me + step, total)), device_id_type=MESH
        )

    fetches[5].wait()
    fetches[6].wait()
    place = lax.broadcasted_iota(jnp.int32, (8, 128), 1)
    numbers = jnp.zeros((8, 128), jnp.int32)
    for n in range(frames_here):
        numbers = jnp.where(place == n, clip_in[0, n], numbers)
    for n in range(frames_here * lat_rows):
        numbers = jnp.where(place == frames_here + n, owner_in[0, n], numbers)
    meta_in[...] = numbers
    meta[t] = numbers
    fetches[0].wait()
    for f in range(frames_here):
        turned = jnp.transpose(act_raw[:, f], (1, 0, 2))
        act[f] = turned
        x[c + f, pl.ds(1, rows), c] = turned

    pl.semaphore_wait(barrier, total - 1)

    def remote(src, dst, send, recv, device):
        return pltpu.make_async_remote_copy(
            src_ref=src, dst_ref=dst, send_sem=send, recv_sem=recv, device_id=device,
            device_id_type=MESH,
        )

    def meta_copy(target):
        return remote(
            meta_in, meta.at[t], meta_send.at[target], meta_recv.at[t],
            {"tm": target, "space": s, "chan": c},
        )

    @pl.loop(1, n_tm)
    def _(step):
        meta_copy(lax.rem(t + step, n_tm)).start()

    up_ok, down_ok = t < n_tm - 1, t > 0
    t_up, t_down = jnp.minimum(t + 1, n_tm - 1), jnp.maximum(t - 1, 0)

    def zrow(up, piece):
        frame, slot, core, tt = (1, 0, 1, t_up) if up else (0, 2, 0, t_down)
        return remote(
            act.at[frame, pl.ds(piece * step_rows, step_rows)],
            x.at[slot, pl.ds(1 + piece * step_rows, step_rows), c],
            zrow_send.at[int(up), piece], zrow_recv.at[c, piece],
            {"tm": tt, "space": s, "chan": core},
        )

    def space_of(low):
        return jnp.maximum(s - 1, 0) if low else jnp.minimum(s + 1, n_space - 1)

    def edge(low, core):
        return remote(
            act.at[:, 0 if low else rows - 1],
            x.at[pl.ds(core, 2), rows + 1 if low else 0, c],
            near_send.at[int(low) * 2 + core], near_recv.at[int(low) * 2 + c],
            {"tm": t, "space": space_of(low), "chan": core},
        )

    def zedge(up, low):
        frame, slot, core, tt = (1, 0, 1, t_up) if up else (0, 2, 0, t_down)
        return remote(
            act.at[frame, 0 if low else rows - 1],
            x.at[slot, rows + 1 if low else 0, c],
            near_send.at[4 + int(low) * 2 + int(up)], near_recv.at[4 + int(low) * 2 + c],
            {"tm": tt, "space": space_of(low), "chan": core},
        )

    peer = remote(
        act, x.at[pl.ds(1 - c, 2), pl.ds(1, rows), c], near_send.at[8], near_recv.at[8],
        {"tm": t, "space": s, "chan": 1 - c},
    )
    low_ok, high_ok = s > 0, s < n_space - 1
    sides = ((True, low_ok), (False, high_ok))
    zs = ((True, up_ok), (False, down_ok))

    peer.start()
    for low, ok in sides:
        for up, z_ok in zs:
            @pl.when(jnp.logical_and(ok, z_ok))
            def _(low=low, up=up):
                zedge(up, low).start()
    for piece in range(chunks):
        for up, z_ok in zs:
            @pl.when(z_ok)
            def _(piece=piece, up=up):
                zrow(up, piece).start()
    for low, ok in sides:
        @pl.when(ok)
        def _(low=low):
            edge(low, 0).start()
            edge(low, 1).start()

    zero_row = jnp.zeros((3, 2, half, columns), BF16)

    @pl.when(s == 0)
    def _():
        x[:, 0] = zero_row

    @pl.when(s == n_space - 1)
    def _():
        x[:, rows + 1] = zero_row

    @pl.when(jnp.logical_and(first, c == 1))
    def _():
        x[0, pl.ds(1, rows)] = jnp.zeros((rows, 2, half, columns), BF16)

        @pl.when(s > 0)
        def _():
            x[0, 0] = zero_row[0]

        @pl.when(s < n_space - 1)
        def _():
            x[0, rows + 1] = zero_row[0]

    for fetch in fetches[1:5]:
        fetch.wait()
    for k in range(3):
        for i in range(3):
            for j in range(3):
                wt[k, pl.ds(j * 128, 128), pl.ds(i * 128, 128)] = weight[k, i, j].T
    gain_c = jnp.broadcast_to(gain[...], (128, 128)).T
    bias_c = jnp.broadcast_to(bias[...], (128, 128)).T * 0.5

    peer.wait_recv()
    for low, ok in ((True, high_ok), (False, low_ok)):
        for core in range(2):
            @pl.when(ok)
            def _(low=low, core=core):
                remote(
                    act.at[:, 0], x.at[pl.ds(c, 2), rows + 1 if low else 0, core],
                    near_send.at[int(low) * 2 + core], near_recv.at[int(low) * 2 + core],
                    {"tm": t, "space": s, "chan": c},
                ).wait_recv()

    lane = lax.broadcasted_iota(jnp.int32, (CHANNELS, columns), 1)

    def conv_row(h, kept, taps):
        acc = None
        for k in range(3):
            term = jnp.dot(wt[k], taps[k](h), preferred_element_type=F32)
            acc = term if acc is None else acc + term
        left = jnp.where(lane == 0, 0.0, pltpu.roll(acc[0:128], 1, 1))
        right = jnp.where(lane == columns - 1, 0.0, pltpu.roll(acc[256:384], columns - 1, 1))
        value = (left + acc[128:256] + right).astype(BF16)
        conv[kept, h] = value
        value = value.astype(F32)
        a, b = value[:, :lanes], value[:, lanes:]
        sums[0] += a + b
        sums[1] += a * a + b * b

    def slab(slot):
        return lambda h: x[slot, pl.ds(h, 3)].reshape(3 * CHANNELS, columns)

    def sums_to(row):
        stat[pl.ds(row, 1), :] = jnp.sum(sums[0].T, axis=0, keepdims=True)
        stat[pl.ds(row + 1, 1), :] = jnp.sum(sums[1].T, axis=0, keepdims=True)

    @pl.when(first)
    def _():
        sums[...] = jnp.zeros_like(sums)

        @pl.loop(c * (rows // 2), (c + 1) * (rows // 2))
        def _(h):
            conv_row(h, 1, [slab(c)] * 3)

        sums_to(2)

    gets_z = jnp.logical_or(jnp.logical_and(c == 1, down_ok), jnp.logical_and(c == 0, up_ok))
    my_frame = 2 * t + 2 - c
    t_near = jnp.where(gets_z, jnp.where(c == 1, t_down, t_up), t)

    @pl.when(gets_z)
    def _():
        remote(
            meta_in, meta.at[t_near], meta_send.at[t_near], meta_recv.at[t_near],
            {"tm": t_near, "space": s, "chan": c},
        ).wait_recv()

    near_ids = pltpu.make_async_copy(meta.at[t_near], ids_near, local_sem.at[8])
    near_ids.start()
    near_ids.wait()
    my_clip = jnp.where(c == 1, clip_in[0, 1], ids_near[0, 0])
    newer = jnp.where(c == 1, clip_in[0, 0], clip_in[0, 1]) == my_clip
    oldest = jnp.where(c == 1, ids_near[0, 1], clip_in[0, 0])
    older = jnp.logical_and(my_frame >= 2, oldest == my_clip)

    z_slot = 2 * (1 - c)

    def wait_zedge(low, ok):
        for core in range(2):
            @pl.when(jnp.logical_and(gets_z, ok))
            def _(core=core):
                remote(
                    act.at[0, 0], x.at[z_slot, rows + 1 if low else 0, core],
                    near_send.at[4 + int(low) * 2], near_recv.at[4 + int(low) * 2 + core],
                    {"tm": t, "space": s, "chan": c},
                ).wait_recv()

    def wait_zrow(piece):
        for core in range(2):
            @pl.when(gets_z)
            def _(core=core):
                remote(
                    act.at[0, pl.ds(piece * step_rows, step_rows)],
                    x.at[z_slot, pl.ds(1 + piece * step_rows, step_rows), core],
                    zrow_send.at[0, piece], zrow_recv.at[core, piece],
                    {"tm": t, "space": s, "chan": c},
                ).wait_recv()

    def tap_old(h):
        return jnp.where(older, slab(0)(h), tap_mid(h))

    def tap_mid(h):
        return jnp.where(newer, slab(1)(h), slab(2)(h))

    taps = [tap_old, tap_mid, slab(2)]
    wait_zedge(False, low_ok)
    wait_zedge(True, high_ok)

    @pl.when(has_main)
    def _():
        sums[...] = jnp.zeros_like(sums)

    for piece in range(chunks):
        wait_zrow(piece)
        begin = 0 if piece == 0 else piece * step_rows - 1
        end = rows if piece == chunks - 1 else (piece + 1) * step_rows - 1

        @pl.when(has_main)
        def _(begin=begin, end=end):
            @pl.loop(begin, end)
            def _(h):
                conv_row(h, 0, taps)

    @pl.when(has_main)
    def _():
        sums_to(0)

    def stat_copy(target):
        return remote(
            stat, stats.at[me], stat_send.at[target], stat_recv.at[me], where_is(target)
        )

    stats[me] = stat[...]

    def near(device):
        return jnp.abs(device // (2 * n_space) - t) <= reach

    @pl.loop(1, total)
    def _(step):
        target = lax.rem(me + step, total)

        @pl.when(near(target))
        def _():
            stat_copy(target).start()

    spread_row = lax.broadcasted_iota(jnp.int32, (columns, columns), 0)
    spread_col = lax.broadcasted_iota(jnp.int32, (columns, columns), 1)
    picked = jnp.where(spread_col < lanes, 2 * spread_col, 2 * (spread_col - lanes) + 1)
    spread = jnp.where(spread_row == picked, 1.0, 0.0).astype(BF16)

    def part_columns(kept, begin, end):
        @pl.loop(begin, end)
        def _(h):
            conv[kept, h] = jnp.dot(
                conv[kept, h], spread, preferred_element_type=F32
            ).astype(BF16)

    @pl.when(has_main)
    def _():
        part_columns(0, 0, rows)

    @pl.when(first)
    def _():
        part_columns(1, c * (rows // 2), (c + 1) * (rows // 2))

    @pl.loop(1, n_tm)
    def _(step):
        source = lax.rem(t + step, n_tm)

        @pl.when(source != t_near)
        def _():
            remote(
                meta_in, meta.at[source], meta_send.at[source], meta_recv.at[source],
                {"tm": source, "space": s, "chan": c},
            ).wait_recv()

    to_scalars = pltpu.make_async_copy(meta, ids, local_sem.at[0])
    to_scalars.start()
    to_scalars.wait()

    def clip_of(frame):
        frame = jnp.minimum(frame, n_frames - 1)
        return ids[frame // 2, 0, frame % 2]

    @pl.loop(1, total)
    def _(step):
        source = lax.rem(me + step, total)

        @pl.when(near(source))
        def _():
            remote(
                stat, stats.at[source], stat_send.at[source], stat_recv.at[source],
                where_is(source),
            ).wait_recv()

    lane8 = lax.broadcasted_iota(jnp.int32, (8, 128), 1)

    def group_sum(v):
        v = v + jnp.where(lane8 % 2 == 0, pltpu.roll(v, 127, 1), pltpu.roll(v, 1, 1))
        return v + jnp.where(lane8 % 4 < 2, pltpu.roll(v, 126, 1), pltpu.roll(v, 2, 1))

    weights = jnp.concatenate([out_weight[q] for q in range(4)], axis=1)

    def moments_of(clip):
        def add_main(source, carry):
            frame = 2 * (source // (2 * n_space)) + 2 - source % 2
            same = jnp.logical_and(frame < n_frames, clip_of(frame) == clip)
            return carry + jnp.where(same, stats[source], 0.0)

        gathered = lax.fori_loop(0, total, add_main, jnp.zeros((8, 128), F32))
        zero_frame = jnp.zeros((8, 128), F32)
        for n in range(2 * n_space):
            zero_frame += stats[n]
        zero_frame = jnp.where(clip_of(0) == clip, zero_frame, 0.0)
        number = jnp.float32(0)
        for frame in range(n_frames):
            number += jnp.where(clip_of(frame) == clip, 1.0, 0.0)
        count = number * float(rows * n_space * columns * GROUP_SIZE)
        gathered = group_sum(gathered)
        zero_frame = group_sum(zero_frame)
        count = jnp.broadcast_to(count, (1, 128))
        mean = (gathered[0:1] + zero_frame[2:3]) / count
        var = (gathered[1:2] + zero_frame[3:4]) / count - mean * mean
        rstd = lax.rsqrt(var + 1e-6)
        mean_c = jnp.broadcast_to(mean, (128, 128)).T
        scale_c = jnp.broadcast_to(rstd, (128, 128)).T * gain_c * 0.5
        return mean_c, scale_c

    def finish(kept, piece, mean_c, scale_c):
        wide = []
        for r in range(piece_rows):
            parts = []
            for i in range(2):
                value = conv[kept, 2 * piece_rows * piece + 2 * r + i].astype(F32)
                for j in range(2):
                    v = (value[:, j * lanes:(j + 1) * lanes] - mean_c) * scale_c + bias_c
                    parts.append((v + v * jnp.tanh(v)).astype(BF16))
            wide.append(jnp.concatenate(parts, axis=0))
        wide = jnp.concatenate(wide, axis=1)
        result = jnp.dot(weights, wide, preferred_element_type=F32).astype(BF16)
        for r in range(piece_rows):
            latent[kept, 0, piece * piece_rows + r] = result[0:16, r * lanes:(r + 1) * lanes]
            latent[kept, 1, piece * piece_rows + r] = result[16:32, r * lanes:(r + 1) * lanes]

    def lat_copy(kept, piece, frame, target, core, send, recv):
        span = pl.ds(piece * piece_rows, piece_rows)
        return remote(
            latent.at[kept, core, span], arrived.at[frame, span], send.at[target * 2 + core], recv,
            {"tm": target, "space": s, "chan": core},
        )

    here = t * 2 + c
    places = n_tm * 2

    def send_latent(kept, piece, frame, send, recv):
        span = pl.ds(piece * piece_rows, piece_rows)
        arrived[frame, span] = latent[kept, c, span]

        @pl.loop(1, places)
        def _(step):
            target = lax.rem(here + step, places)
            lat_copy(kept, piece, frame, target // 2, target % 2, send, recv).start()

    @pl.when(first)
    def _():
        finish(1, c, *moments_of(clip_of(0)))
        send_latent(1, c, 0, extra_send, extra_recv.at[c])

    @pl.when(has_main)
    def _():
        found = moments_of(my_clip)
        for piece in range(2):
            finish(0, piece, *found)
            send_latent(0, piece, my_frame, lat_send.at[piece], lat_recv.at[my_frame, piece])

    @pl.loop(1, n_frames)
    def _(frame):
        @pl.when(frame != my_frame)
        def _():
            for piece in range(2):
                lat_copy(
                    0, piece, frame, t, c, lat_send.at[piece], lat_recv.at[frame, piece]
                ).wait_recv()

    for piece in range(2):
        @pl.when(jnp.logical_not(jnp.logical_and(first, c == piece)))
        def _(piece=piece):
            lat_copy(0, piece, 0, t, c, lat_send.at[piece], extra_recv.at[piece]).wait_recv()

    @pl.loop(0, n_tm)
    def _(b):
        taken = jnp.int32(0)
        slots = []
        for n in range(2 * lat_rows):
            hit = ids[b, 0, frames_here + n] == t
            slots.append(jnp.where(hit, taken, -1))
            taken = taken + jnp.where(hit, 1, 0)
        for j in range(capacity):
            value = jnp.zeros((16, lanes), BF16)
            for n in range(2 * lat_rows):
                row = arrived[2 * b + n // lat_rows, n % lat_rows]
                value = jnp.where(slots[n] == j, row, value)
            out[0, b * capacity + j] = value

    @pl.loop(1, n_tm)
    def _(step):
        meta_copy(lax.rem(t + step, n_tm)).wait_send()

    peer.wait_send()
    for low, ok in sides:
        for up, z_ok in zs:
            @pl.when(jnp.logical_and(ok, z_ok))
            def _(low=low, up=up):
                zedge(up, low).wait_send()

        @pl.when(ok)
        def _(low=low):
            edge(low, 0).wait_send()
            edge(low, 1).wait_send()
    for piece in range(chunks):
        for up, z_ok in zs:
            @pl.when(z_ok)
            def _(piece=piece, up=up):
                zrow(up, piece).wait_send()

    @pl.loop(1, total)
    def _(step):
        target = lax.rem(me + step, total)

        @pl.when(near(target))
        def _():
            stat_copy(target).wait_send()

    def latents_left(kept, piece, frame, send, recv):
        @pl.loop(1, places)
        def _(step):
            target = lax.rem(here + step, places)
            lat_copy(kept, piece, frame, target // 2, target % 2, send, recv).wait_send()

    @pl.when(first)
    def _():
        latents_left(1, c, 0, extra_send, extra_recv.at[c])

    @pl.when(has_main)
    def _():
        for piece in range(2):
            latents_left(0, piece, my_frame, lat_send.at[piece], lat_recv.at[my_frame, piece])


def solution(mesh):
    n_tm, n_space = mesh.shape["tm"], mesh.shape["space"]
    total = n_tm * n_space * 2

    def shards(activations, frame_clip, conv_weight, norm_gain, norm_bias, out_weight, owner):
        half, frames_here, rows, columns = activations.shape
        lat_rows = rows // 2
        capacity = max(2, 2 * frames_here * lat_rows // n_tm)
        chunks = rows
        moments = out_weight.shape[-1]
        dma = pltpu.SemaphoreType.DMA
        return pl.pallas_call(
            functools.partial(kernel, (n_tm, n_space, capacity, chunks)),
            out_shape=jax.ShapeDtypeStruct(
                (1, n_tm * capacity, moments // 2, columns // 2), BF16
            ),
            in_specs=[pl.BlockSpec(memory_space=pltpu.HBM)] * 7,
            out_specs=pl.BlockSpec(memory_space=pltpu.VMEM),
            scratch_shapes=[
                pltpu.SMEM((1, frames_here), jnp.int32),
                pltpu.SMEM((1, frames_here * lat_rows), jnp.int32),
                pltpu.VMEM(activations.shape, BF16),
                pltpu.VMEM((frames_here, rows, half, columns), BF16),
                pltpu.VMEM(conv_weight.shape, BF16),
                pltpu.VMEM((1, CHANNELS), F32),
                pltpu.VMEM((1, CHANNELS), F32),
                pltpu.VMEM((4, moments, CHANNELS), BF16),
                pltpu.VMEM((8, 128), jnp.int32),
                pltpu.VMEM((3, rows + 2, 2, half, columns), BF16),
                pltpu.VMEM((3, 384, 384), BF16),
                pltpu.VMEM((2, rows, CHANNELS, columns), BF16),
                pltpu.VMEM((8, 128), F32),
                pltpu.VMEM((total, 8, 128), F32),
                pltpu.VMEM((2, 2, lat_rows, moments // 2, columns // 2), BF16),
                pltpu.VMEM((n_tm * frames_here, lat_rows, moments // 2, columns // 2), BF16),
                pltpu.VMEM((n_tm, 8, 128), jnp.int32),
                pltpu.SMEM((n_tm, 8, 128), jnp.int32),
                pltpu.SMEM((8, 128), jnp.int32),
                pltpu.VMEM((2, CHANNELS, columns // 2), F32),
                dma((9,)),
                dma((9,)),
                dma((2, chunks)),
                dma((2, chunks)),
                dma((n_tm,)),
                dma((n_tm,)),
                dma((total,)),
                dma((total,)),
                dma((2, 2 * n_tm)),
                dma((n_tm * frames_here, 2)),
                dma((2 * n_tm,)),
                dma((2,)),
                dma((9,)),
            ],
            compiler_params=pltpu.CompilerParams(
                collective_id=0, has_side_effects=True, vmem_limit_bytes=67_043_328
            ),
        )(
            frame_clip.reshape(1, -1), owner.reshape(1, -1), activations, conv_weight,
            norm_gain.reshape(1, -1), norm_bias.reshape(1, -1),
            out_weight.transpose(0, 1, 3, 2).reshape(4, moments, CHANNELS),
        )

    placed = (
        P(("groups", "chan"), "tm", "space", None),
        P(("groups", "tm")),
        P(),
        P(),
        P(),
        P(),
        P(("groups", "space"), "tm", None),
    )
    return jax.shard_map(
        shards,
        mesh=mesh,
        in_specs=placed,
        out_specs=P(("groups", "space"), "tm", "chan", None),
        check_vma=False,
    )
```

```python
import functools

import jax
import jax.numpy as jnp
from jax import lax
from jax.experimental import pallas as pl
from jax.experimental.pallas import tpu as pltpu
from jax.sharding import PartitionSpec as P

CHANNELS = 128
GROUPS = 32
GROUP_SIZE = CHANNELS // GROUPS
F32 = jnp.float32
BF16 = jnp.bfloat16
MESH = pl.DeviceIdType.MESH


def kernel(
    sizes, clip_hbm, owner_hbm, act_in, weight_in, gain_in, bias_in, out_weight_in, out,
    clip_in, owner_in, act_raw, act, weight, gain, bias, out_weight, meta_in,
    x, wt, conv, stat, stats, latent, arrived, meta, ids, ids_near, sums,
    near_send, near_recv, zrow_send, zrow_recv, meta_send, meta_recv, stat_send, stat_recv,
    lat_send, lat_recv, extra_send, extra_recv, local_sem,
):
    n_tm, n_space, capacity, chunks = sizes
    frames_here, rows, half, columns = act.shape
    lanes = columns // 2
    total = n_tm * n_space * 2
    n_frames = n_tm * frames_here
    lat_rows = rows // 2
    step_rows = rows // chunks
    t = lax.axis_index("tm")
    s = lax.axis_index("space")
    c = lax.axis_index("chan")
    me = (t * n_space + s) * 2 + c
    first = t == 0
    piece_rows = lat_rows // 2
    reach = n_tm // 2
    has_main = jnp.logical_or(c == 1, t < n_tm - 1)

    def where_is(flat):
        return {"tm": flat // (2 * n_space), "space": (flat // 2) % n_space, "chan": flat % 2}

    fetches = [
        pltpu.make_async_copy(source, held, local_sem.at[1 + n])
        for n, (source, held) in enumerate((
            (act_in, act_raw), (weight_in, weight), (gain_in, gain), (bias_in, bias),
            (out_weight_in, out_weight),
            (clip_hbm, clip_in), (owner_hbm, owner_in),
        ))
    ]
    for fetch in fetches:
        fetch.start()
    stats[...] = jnp.zeros_like(stats)
    stat[...] = jnp.zeros_like(stat)

    barrier = pltpu.get_barrier_semaphore()

    @pl.loop(1, total)
    def _(step):
        pl.semaphore_signal(
            barrier, inc=1, device_id=where_is(lax.rem(me + step, total)), device_id_type=MESH
        )

    fetches[5].wait()
    fetches[6].wait()
    place = lax.broadcasted_iota(jnp.int32, (8, 128), 1)
    numbers = jnp.zeros((8, 128), jnp.int32)
    for n in range(frames_here):
        numbers = jnp.where(place == n, clip_in[0, n], numbers)
    for n in range(frames_here * lat_rows):
        numbers = jnp.where(place == frames_here + n, owner_in[0, n], numbers)
    meta_in[...] = numbers
    meta[t] = numbers
    fetches[0].wait()
    for f in range(frames_here):
        turned = jnp.transpose(act_raw[:, f], (1, 0, 2))
        act[f] = turned
        x[c + f, pl.ds(1, rows), c] = turned

    pl.semaphore_wait(barrier, total - 1)

    def remote(src, dst, send, recv, device):
        return pltpu.make_async_remote_copy(
            src_ref=src, dst_ref=dst, send_sem=send, recv_sem=recv, device_id=device,
            device_id_type=MESH,
        )

    def meta_copy(target):
        return remote(
            meta_in, meta.at[t], meta_send.at[target], meta_recv.at[t],
            {"tm": target, "space": s, "chan": c},
        )

    @pl.loop(1, n_tm)
    def _(step):
        meta_copy(lax.rem(t + step, n_tm)).start()

    up_ok, down_ok = t < n_tm - 1, t > 0
    t_up, t_down = jnp.minimum(t + 1, n_tm - 1), jnp.maximum(t - 1, 0)

    def zrow(up, piece):
        frame, slot, core, tt = (1, 0, 1, t_up) if up else (0, 2, 0, t_down)
        return remote(
            act.at[frame, pl.ds(piece * step_rows, step_rows)],
            x.at[slot, pl.ds(1 + piece * step_rows, step_rows), c],
            zrow_send.at[int(up), piece], zrow_recv.at[c, piece],
            {"tm": tt, "space": s, "chan": core},
        )

    def space_of(low):
        return jnp.maximum(s - 1, 0) if low else jnp.minimum(s + 1, n_space - 1)

    def edge(low, core):
        return remote(
            act.at[:, 0 if low else rows - 1],
            x.at[pl.ds(core, 2), rows + 1 if low else 0, c],
            near_send.at[int(low) * 2 + core], near_recv.at[int(low) * 2 + c],
            {"tm": t, "space": space_of(low), "chan": core},
        )

    def zedge(up, low):
        frame, slot, core, tt = (1, 0, 1, t_up) if up else (0, 2, 0, t_down)
        return remote(
            act.at[frame, 0 if low else rows - 1],
            x.at[slot, rows + 1 if low else 0, c],
            near_send.at[4 + int(low) * 2 + int(up)], near_recv.at[4 + int(low) * 2 + c],
            {"tm": tt, "space": space_of(low), "chan": core},
        )

    peer = remote(
        act, x.at[pl.ds(1 - c, 2), pl.ds(1, rows), c], near_send.at[8], near_recv.at[8],
        {"tm": t, "space": s, "chan": 1 - c},
    )
    low_ok, high_ok = s > 0, s < n_space - 1
    sides = ((True, low_ok), (False, high_ok))
    zs = ((True, up_ok), (False, down_ok))

    for low, ok in sides:
        for up, z_ok in zs:
            @pl.when(jnp.logical_and(ok, z_ok))
            def _(low=low, up=up):
                zedge(up, low).start()
    for piece in range(chunks):
        for up, z_ok in zs:
            @pl.when(z_ok)
            def _(piece=piece, up=up):
                zrow(up, piece).start()
    for low, ok in sides:
        @pl.when(ok)
        def _(low=low):
            edge(low, 0).start()
            edge(low, 1).start()

    peer.start()

    zero_row = jnp.zeros((3, 2, half, columns), BF16)

    @pl.when(s == 0)
    def _():
        x[:, 0] = zero_row

    @pl.when(s == n_space - 1)
    def _():
        x[:, rows + 1] = zero_row

    @pl.when(jnp.logical_and(first, c == 1))
    def _():
        x[0, pl.ds(1, rows)] = jnp.zeros((rows, 2, half, columns), BF16)

        @pl.when(s > 0)
        def _():
            x[0, 0] = zero_row[0]

        @pl.when(s < n_space - 1)
        def _():
            x[0, rows + 1] = zero_row[0]

    for fetch in fetches[1:5]:
        fetch.wait()
    for k in range(3):
        for i in range(3):
            for j in range(3):
                wt[k, pl.ds(j * 128, 128), pl.ds(i * 128, 128)] = weight[k, i, j].T
    gain_c = jnp.broadcast_to(gain[...], (128, 128)).T
    bias_c = jnp.broadcast_to(bias[...], (128, 128)).T * 0.5

    peer.wait_recv()
    for low, ok in ((True, high_ok), (False, low_ok)):
        for core in range(2):
            @pl.when(ok)
            def _(low=low, core=core):
                remote(
                    act.at[:, 0], x.at[pl.ds(c, 2), rows + 1 if low else 0, core],
                    near_send.at[int(low) * 2 + core], near_recv.at[int(low) * 2 + core],
                    {"tm": t, "space": s, "chan": c},
                ).wait_recv()

    lane = lax.broadcasted_iota(jnp.int32, (CHANNELS, columns), 1)

    def conv_row(h, kept, taps):
        acc = None
        for k in range(3):
            term = jnp.dot(wt[k], taps[k](h), preferred_element_type=F32)
            acc = term if acc is None else acc + term
        left = jnp.where(lane == 0, 0.0, pltpu.roll(acc[0:128], 1, 1))
        right = jnp.where(lane == columns - 1, 0.0, pltpu.roll(acc[256:384], columns - 1, 1))
        value = (left + acc[128:256] + right).astype(BF16)
        conv[kept, h] = value
        value = value.astype(F32)
        a, b = value[:, :lanes], value[:, lanes:]
        sums[0] += a + b
        sums[1] += a * a + b * b

    def slab(slot):
        return lambda h: x[slot, pl.ds(h, 3)].reshape(3 * CHANNELS, columns)

    def sums_to(row):
        stat[pl.ds(row, 1), :] = jnp.sum(sums[0].T, axis=0, keepdims=True)
        stat[pl.ds(row + 1, 1), :] = jnp.sum(sums[1].T, axis=0, keepdims=True)

    @pl.when(first)
    def _():
        sums[...] = jnp.zeros_like(sums)

        @pl.loop(c * (rows // 2), (c + 1) * (rows // 2))
        def _(h):
            conv_row(h, 1, [slab(c)] * 3)

        sums_to(2)

    gets_z = jnp.logical_or(jnp.logical_and(c == 1, down_ok), jnp.logical_and(c == 0, up_ok))
    my_frame = 2 * t + 2 - c
    t_near = jnp.where(gets_z, jnp.where(c == 1, t_down, t_up), t)

    @pl.when(gets_z)
    def _():
        remote(
            meta_in, meta.at[t_near], meta_send.at[t_near], meta_recv.at[t_near],
            {"tm": t_near, "space": s, "chan": c},
        ).wait_recv()

    near_ids = pltpu.make_async_copy(meta.at[t_near], ids_near, local_sem.at[8])
    near_ids.start()
    near_ids.wait()
    my_clip = jnp.where(c == 1, clip_in[0, 1], ids_near[0, 0])
    newer = jnp.where(c == 1, clip_in[0, 0], clip_in[0, 1]) == my_clip
    oldest = jnp.where(c == 1, ids_near[0, 1], clip_in[0, 0])
    older = jnp.logical_and(my_frame >= 2, oldest == my_clip)

    z_slot = 2 * (1 - c)

    def wait_zedge(low, ok):
        for core in range(2):
            @pl.when(jnp.logical_and(gets_z, ok))
            def _(core=core):
                remote(
                    act.at[0, 0], x.at[z_slot, rows + 1 if low else 0, core],
                    near_send.at[4 + int(low) * 2], near_recv.at[4 + int(low) * 2 + core],
                    {"tm": t, "space": s, "chan": c},
                ).wait_recv()

    def wait_zrow(piece):
        for core in range(2):
            @pl.when(gets_z)
            def _(core=core):
                remote(
                    act.at[0, pl.ds(piece * step_rows, step_rows)],
                    x.at[z_slot, pl.ds(1 + piece * step_rows, step_rows), core],
                    zrow_send.at[0, piece], zrow_recv.at[core, piece],
                    {"tm": t, "space": s, "chan": c},
                ).wait_recv()

    def tap_old(h):
        return jnp.where(older, slab(0)(h), tap_mid(h))

    def tap_mid(h):
        return jnp.where(newer, slab(1)(h), slab(2)(h))

    taps = [tap_old, tap_mid, slab(2)]
    wait_zedge(False, low_ok)
    wait_zedge(True, high_ok)

    @pl.when(has_main)
    def _():
        sums[...] = jnp.zeros_like(sums)

    for piece in range(chunks):
        wait_zrow(piece)
        begin = 0 if piece == 0 else piece * step_rows - 1
        end = rows if piece == chunks - 1 else (piece + 1) * step_rows - 1

        @pl.when(has_main)
        def _(begin=begin, end=end):
            @pl.loop(begin, end)
            def _(h):
                conv_row(h, 0, taps)

    @pl.when(has_main)
    def _():
        sums_to(0)

    def stat_copy(target):
        return remote(
            stat, stats.at[me], stat_send.at[target], stat_recv.at[me], where_is(target)
        )

    stats[me] = stat[...]

    def near(device):
        return jnp.abs(device // (2 * n_space) - t) <= reach

    @pl.loop(1, total)
    def _(step):
        target = lax.rem(me + step, total)

        @pl.when(near(target))
        def _():
            stat_copy(target).start()

    spread_row = lax.broadcasted_iota(jnp.int32, (columns, columns), 0)
    spread_col = lax.broadcasted_iota(jnp.int32, (columns, columns), 1)
    picked = jnp.where(spread_col < lanes, 2 * spread_col, 2 * (spread_col - lanes) + 1)
    spread = jnp.where(spread_row == picked, 1.0, 0.0).astype(BF16)

    def part_columns(kept, begin, end):
        @pl.loop(begin, end)
        def _(h):
            conv[kept, h] = jnp.dot(
                conv[kept, h], spread, preferred_element_type=F32
            ).astype(BF16)

    @pl.when(has_main)
    def _():
        part_columns(0, 0, rows)

    @pl.when(first)
    def _():
        part_columns(1, c * (rows // 2), (c + 1) * (rows // 2))

    @pl.loop(1, n_tm)
    def _(step):
        source = lax.rem(t + step, n_tm)

        @pl.when(source != t_near)
        def _():
            remote(
                meta_in, meta.at[source], meta_send.at[source], meta_recv.at[source],
                {"tm": source, "space": s, "chan": c},
            ).wait_recv()

    to_scalars = pltpu.make_async_copy(meta, ids, local_sem.at[0])
    to_scalars.start()
    to_scalars.wait()

    def clip_of(frame):
        frame = jnp.minimum(frame, n_frames - 1)
        return ids[frame // 2, 0, frame % 2]

    @pl.loop(1, total)
    def _(step):
        source = lax.rem(me + step, total)

        @pl.when(near(source))
        def _():
            remote(
                stat, stats.at[source], stat_send.at[source], stat_recv.at[source],
                where_is(source),
            ).wait_recv()

    lane8 = lax.broadcasted_iota(jnp.int32, (8, 128), 1)

    def group_sum(v):
        v = v + jnp.where(lane8 % 2 == 0, pltpu.roll(v, 127, 1), pltpu.roll(v, 1, 1))
        return v + jnp.where(lane8 % 4 < 2, pltpu.roll(v, 126, 1), pltpu.roll(v, 2, 1))

    weights = jnp.concatenate([out_weight[q] for q in range(4)], axis=1)

    def moments_of(clip):
        def add_main(source, carry):
            frame = 2 * (source // (2 * n_space)) + 2 - source % 2
            same = jnp.logical_and(frame < n_frames, clip_of(frame) == clip)
            return carry + jnp.where(same, stats[source], 0.0)

        gathered = lax.fori_loop(0, total, add_main, jnp.zeros((8, 128), F32))
        zero_frame = jnp.zeros((8, 128), F32)
        for n in range(2 * n_space):
            zero_frame += stats[n]
        zero_frame = jnp.where(clip_of(0) == clip, zero_frame, 0.0)
        number = jnp.float32(0)
        for frame in range(n_frames):
            number += jnp.where(clip_of(frame) == clip, 1.0, 0.0)
        count = number * float(rows * n_space * columns * GROUP_SIZE)
        gathered = group_sum(gathered)
        zero_frame = group_sum(zero_frame)
        count = jnp.broadcast_to(count, (1, 128))
        mean = (gathered[0:1] + zero_frame[2:3]) / count
        var = (gathered[1:2] + zero_frame[3:4]) / count - mean * mean
        rstd = lax.rsqrt(var + 1e-6)
        mean_c = jnp.broadcast_to(mean, (128, 128)).T
        scale_c = jnp.broadcast_to(rstd, (128, 128)).T * gain_c * 0.5
        return mean_c, scale_c

    def finish(kept, piece, mean_c, scale_c):
        wide = []
        for r in range(piece_rows):
            parts = []
            for i in range(2):
                value = conv[kept, 2 * piece_rows * piece + 2 * r + i].astype(F32)
                for j in range(2):
                    v = (value[:, j * lanes:(j + 1) * lanes] - mean_c) * scale_c + bias_c
                    parts.append((v + v * jnp.tanh(v)).astype(BF16))
            wide.append(jnp.concatenate(parts, axis=0))
        wide = jnp.concatenate(wide, axis=1)
        result = jnp.dot(weights, wide, preferred_element_type=F32).astype(BF16)
        for r in range(piece_rows):
            latent[kept, 0, piece * piece_rows + r] = result[0:16, r * lanes:(r + 1) * lanes]
            latent[kept, 1, piece * piece_rows + r] = result[16:32, r * lanes:(r + 1) * lanes]

    def lat_copy(kept, piece, frame, target, core, send, recv):
        span = pl.ds(piece * piece_rows, piece_rows)
        return remote(
            latent.at[kept, core, span], arrived.at[frame, span], send.at[target * 2 + core], recv,
            {"tm": target, "space": s, "chan": core},
        )

    here = t * 2 + c
    places = n_tm * 2

    def send_latent(kept, piece, frame, send, recv):
        span = pl.ds(piece * piece_rows, piece_rows)
        arrived[frame, span] = latent[kept, c, span]

        @pl.loop(1, places)
        def _(step):
            target = lax.rem(here + step, places)
            lat_copy(kept, piece, frame, target // 2, target % 2, send, recv).start()

    @pl.when(first)
    def _():
        finish(1, c, *moments_of(clip_of(0)))
        send_latent(1, c, 0, extra_send, extra_recv.at[c])

    @pl.when(has_main)
    def _():
        found = moments_of(my_clip)
        for piece in range(2):
            finish(0, piece, *found)
            send_latent(0, piece, my_frame, lat_send.at[piece], lat_recv.at[my_frame, piece])

    @pl.loop(1, n_frames)
    def _(frame):
        @pl.when(frame != my_frame)
        def _():
            for piece in range(2):
                lat_copy(
                    0, piece, frame, t, c, lat_send.at[piece], lat_recv.at[frame, piece]
                ).wait_recv()

    for piece in range(2):
        @pl.when(jnp.logical_not(jnp.logical_and(first, c == piece)))
        def _(piece=piece):
            lat_copy(0, piece, 0, t, c, lat_send.at[piece], extra_recv.at[piece]).wait_recv()

    @pl.loop(0, n_tm)
    def _(b):
        taken = jnp.int32(0)
        slots = []
        for n in range(2 * lat_rows):
            hit = ids[b, 0, frames_here + n] == t
            slots.append(jnp.where(hit, taken, -1))
            taken = taken + jnp.where(hit, 1, 0)
        for j in range(capacity):
            value = jnp.zeros((16, lanes), BF16)
            for n in range(2 * lat_rows):
                row = arrived[2 * b + n // lat_rows, n % lat_rows]
                value = jnp.where(slots[n] == j, row, value)
            out[0, b * capacity + j] = value

    @pl.loop(1, n_tm)
    def _(step):
        meta_copy(lax.rem(t + step, n_tm)).wait_send()

    peer.wait_send()
    for low, ok in sides:
        for up, z_ok in zs:
            @pl.when(jnp.logical_and(ok, z_ok))
            def _(low=low, up=up):
                zedge(up, low).wait_send()

        @pl.when(ok)
        def _(low=low):
            edge(low, 0).wait_send()
            edge(low, 1).wait_send()
    for piece in range(chunks):
        for up, z_ok in zs:
            @pl.when(z_ok)
            def _(piece=piece, up=up):
                zrow(up, piece).wait_send()

    @pl.loop(1, total)
    def _(step):
        target = lax.rem(me + step, total)

        @pl.when(near(target))
        def _():
            stat_copy(target).wait_send()

    def latents_left(kept, piece, frame, send, recv):
        @pl.loop(1, places)
        def _(step):
            target = lax.rem(here + step, places)
            lat_copy(kept, piece, frame, target // 2, target % 2, send, recv).wait_send()

    @pl.when(first)
    def _():
        latents_left(1, c, 0, extra_send, extra_recv.at[c])

    @pl.when(has_main)
    def _():
        for piece in range(2):
            latents_left(0, piece, my_frame, lat_send.at[piece], lat_recv.at[my_frame, piece])


def solution(mesh):
    n_tm, n_space = mesh.shape["tm"], mesh.shape["space"]
    total = n_tm * n_space * 2

    def shards(activations, frame_clip, conv_weight, norm_gain, norm_bias, out_weight, owner):
        half, frames_here, rows, columns = activations.shape
        lat_rows = rows // 2
        capacity = max(2, 2 * frames_here * lat_rows // n_tm)
        chunks = 2
        moments = out_weight.shape[-1]
        dma = pltpu.SemaphoreType.DMA
        return pl.pallas_call(
            functools.partial(kernel, (n_tm, n_space, capacity, chunks)),
            out_shape=jax.ShapeDtypeStruct(
                (1, n_tm * capacity, moments // 2, columns // 2), BF16
            ),
            in_specs=[pl.BlockSpec(memory_space=pltpu.HBM)] * 7,
            out_specs=pl.BlockSpec(memory_space=pltpu.VMEM),
            scratch_shapes=[
                pltpu.SMEM((1, frames_here), jnp.int32),
                pltpu.SMEM((1, frames_here * lat_rows), jnp.int32),
                pltpu.VMEM(activations.shape, BF16),
                pltpu.VMEM((frames_here, rows, half, columns), BF16),
                pltpu.VMEM(conv_weight.shape, BF16),
                pltpu.VMEM((1, CHANNELS), F32),
                pltpu.VMEM((1, CHANNELS), F32),
                pltpu.VMEM((4, moments, CHANNELS), BF16),
                pltpu.VMEM((8, 128), jnp.int32),
                pltpu.VMEM((3, rows + 2, 2, half, columns), BF16),
                pltpu.VMEM((3, 384, 384), BF16),
                pltpu.VMEM((2, rows, CHANNELS, columns), BF16),
                pltpu.VMEM((8, 128), F32),
                pltpu.VMEM((total, 8, 128), F32),
                pltpu.VMEM((2, 2, lat_rows, moments // 2, columns // 2), BF16),
                pltpu.VMEM((n_tm * frames_here, lat_rows, moments // 2, columns // 2), BF16),
                pltpu.VMEM((n_tm, 8, 128), jnp.int32),
                pltpu.SMEM((n_tm, 8, 128), jnp.int32),
                pltpu.SMEM((8, 128), jnp.int32),
                pltpu.VMEM((2, CHANNELS, columns // 2), F32),
                dma((9,)),
                dma((9,)),
                dma((2, chunks)),
                dma((2, chunks)),
                dma((n_tm,)),
                dma((n_tm,)),
                dma((total,)),
                dma((total,)),
                dma((2, 2 * n_tm)),
                dma((n_tm * frames_here, 2)),
                dma((2 * n_tm,)),
                dma((2,)),
                dma((9,)),
            ],
            compiler_params=pltpu.CompilerParams(
                collective_id=0, has_side_effects=True, vmem_limit_bytes=66_850_000
            ),
        )(
            frame_clip.reshape(1, -1), owner.reshape(1, -1), activations, conv_weight,
            norm_gain.reshape(1, -1), norm_bias.reshape(1, -1),
            out_weight.transpose(0, 1, 3, 2).reshape(4, moments, CHANNELS),
        )

    placed = (
        P(("groups", "chan"), "tm", "space", None),
        P(("groups", "tm")),
        P(),
        P(),
        P(),
        P(),
        P(("groups", "space"), "tm", None),
    )
    return jax.shard_map(
        shards,
        mesh=mesh,
        in_specs=placed,
        out_specs=P(("groups", "space"), "tm", "chan", None),
        check_vma=False,
    )
```
